32 devices in a mesh: sector: 4 (over x, core), op: 8 (over z, y).
Axes of the slice: x: 2, y: 2, z: 4, core: 2. Of those that a mesh axis runs over, the one named last changes fastest.
Arguments:
- wavefunction: bfloat16 [8, 512, 512], P('sector', 'op'), may hold values from -6 to 6
- sector_bases: bfloat16 [8, 512, 512], P('sector', 'op'), may hold values from -1 to 1
- left_env: bfloat16 [192, 512, 512], P(('sector', 'op')), may hold values from -0.25 to 0.25
- right_env: bfloat16 [192, 512, 512], P(('sector', 'op')), may hold values from -0.0546875 to 0.0546875
- pair_source: int32 [192], P(('sector', 'op')), may hold values from 0 to 7, as said below
- pair_target: int32 [192], P(('sector', 'op')), may hold values from 0 to 7
- sector_slot: int32 [8], replicated, may hold values from 0 to 7, as said below
- orders: int32 [8], replicated, may hold values from 256 to 512, as said below
Outputs:
- sigma_blocks: bfloat16 [8, 512, 512], P('sector', 'op')
- left_rotated: bfloat16 [192, 512, 512], P(('sector', 'op'))
The draws below stay inside these ranges and needn't reach their ends.
Inputs may be any that keep to these rules, and one draw needn't show every extreme that they name: A permutation: sector s's blocks stand at slot sector_slot[s]. `pair_source`: the pairs held by index i of the sector axis have sources whose slots lie in i * 2 to (i + 1) * 2 - 1. `orders`: some sector has order exactly 512.
All inputs are finite; a program needn't handle non-finite values.
Results may differ from the reference program's by a relative error of at most 0.0049.
Values may be sent and summed in bfloat16 or wider, within the bound.
A program may use at most 128 MiB of HBM per device.

```python
import jax
import jax.numpy as jnp
from jax import lax

K = 512
SEC_DEV = 2
PAIRS_DEV = 6
SECTORS = 8
PAIRS = 192
N_SECTOR = 4
N_OP = 8


def slot_table(key):
    return jax.random.permutation(jax.random.fold_in(key, 11), SECTORS).astype(jnp.int32)


def draw_sector_slot(key, part):
    return slot_table(key)


def draw_pair_source(key, part):
    table = slot_table(key)
    sector_of = jnp.argsort(table, stable=True).astype(jnp.int32)
    numbers = jnp.arange(PAIRS, dtype=jnp.int32)
    owner_ids = numbers // (PAIRS // N_SECTOR)
    picks = jax.random.randint(jax.random.fold_in(key, 12), (PAIRS,), 0, SEC_DEV, dtype=jnp.int32)
    return sector_of[owner_ids * SEC_DEV + picks]


def draw_orders(key, part):
    base = jax.random.randint(jax.random.fold_in(key, 14), (SECTORS,), K // 2, K + 1, dtype=jnp.int32)
    marked = jax.random.randint(jax.random.fold_in(key, 15), (), 0, SECTORS, dtype=jnp.int32)
    labels = jnp.arange(SECTORS, dtype=jnp.int32)
    return jnp.where(labels == marked, K, base).astype(jnp.int32)


def plant(drawn, rng, low, largest):
    index_at = [jax.random.randint(jax.random.fold_in(rng, axis), (), 0, length) for axis, length in enumerate(drawn.shape)]
    main_axis = drawn.shape.index(max(drawn.shape))
    neighbour = index_at[:main_axis] + [(index_at[main_axis] + 1) % drawn.shape[main_axis]] + index_at[main_axis + 1:]
    return drawn.at[tuple(index_at)].set(low).at[tuple(neighbour)].set(largest)


def steps_of(stream_key, shape, pieces, low, top_value):
    def one(position, parts):
        heights = jax.random.uniform(jax.random.fold_in(jax.random.fold_in(stream_key, 6), position), (parts,), jnp.float32, low / len(pieces), top_value / len(pieces))
        return jnp.repeat(jnp.exp(heights), shape[position] // parts).reshape((-1,) + (1,) * (len(shape) - position - 1))

    gain = one(*pieces[0])
    for cut in pieces[1:]:
        gain = gain * one(*cut)
    return gain


def gaussian(key, shape, spread, limit, pieces=(), kind=jnp.bfloat16):
    loudness = steps_of(key, shape, pieces, -0.22, 0.18) if pieces else 1.0
    values = jax.random.normal(key, shape, jnp.float32) * spread * loudness
    return jnp.minimum(jnp.maximum(values, -limit), limit).astype(kind)


def setup_inputs(seed: int = 0) -> dict:
    seeds = jax.random.split(jax.random.key(seed), 9)
    return {
        "wavefunction": gaussian(seeds[0], (SECTORS, K, K), 1.0, 6.0, ((0, 4), (1, 8))),
        "sector_bases": gaussian(seeds[1], (SECTORS, K, K), (K // 16) ** -0.5, 1.0, ((0, 4), (1, 8))),
        "left_env": gaussian(seeds[2], (PAIRS, K, K), K ** -0.5, 0.25, ((0, 32),)),
        "right_env": gaussian(seeds[3], (PAIRS, K, K), (K * PAIRS_DEV * N_OP // SEC_DEV) ** -0.5, 0.0546875, ((0, 32),)),
        "pair_source": draw_pair_source(jax.random.fold_in(seeds[8], 71), 0),
        "pair_target": plant(jax.random.randint(seeds[5], (PAIRS,), 0, SECTORS), jax.random.fold_in(seeds[5], 1), 0, SECTORS - 1).astype(jnp.int32),
        "sector_slot": draw_sector_slot(jax.random.fold_in(seeds[8], 71), 0),
        "orders": draw_orders(jax.random.fold_in(seeds[8], 71), 0),
    }


def reference(wavefunction, sector_bases, left_env, right_env, pair_source, pair_target, sector_slot, orders):
    sectors = orders.shape[0]
    width = wavefunction.shape[1]
    slot_order = jnp.zeros((sectors,), jnp.int32).at[sector_slot].set(orders)
    positions = jnp.arange(width, dtype=jnp.int32)
    edge = positions[None, :] < slot_order[:, None]
    inside = edge[:, :, None] & edge[:, None, :]
    masked = jnp.where(inside, wavefunction, jnp.zeros((), wavefunction.dtype))
    source_slot = sector_slot[pair_source].astype(jnp.int32)
    target_slot = sector_slot[pair_target].astype(jnp.int32)

    def apply_pair(totals, entry):
        left_block, right_block, source_at, target_at = entry
        projected = jnp.dot(left_block, masked[source_at], preferred_element_type=jnp.float32).astype(jnp.bfloat16)
        product = jnp.dot(projected, right_block.T, preferred_element_type=jnp.float32)
        totals = totals.at[target_at].add(product)
        half_rotated = jnp.dot(left_block, sector_bases[source_at], preferred_element_type=jnp.float32).astype(jnp.bfloat16)
        rotated = jnp.dot(sector_bases[target_at].T, half_rotated, preferred_element_type=jnp.float32).astype(jnp.bfloat16)
        return totals, rotated

    start_sum = jnp.zeros((sectors, width, width), jnp.float32)
    totals, left_rotated = lax.scan(apply_pair, start_sum, (left_env, right_env, source_slot, target_slot))
    sigma_blocks = jnp.where(inside, totals, jnp.zeros((), jnp.float32)).astype(jnp.bfloat16)
    return sigma_blocks, left_rotated
```

```python
import functools

import jax
import jax.numpy as jnp
from jax import lax
from jax.experimental import pallas as pl
from jax.experimental.pallas import tpu as pltpu
from jax.sharding import PartitionSpec as P

MESH = pl.DeviceIdType.MESH
ANY = pl.BlockSpec(memory_space=pl.ANY)
VMEM = pl.BlockSpec(memory_space=pltpu.VMEM)
SMEM = pl.BlockSpec(memory_space=pltpu.SMEM)


def grid_of(n_sector, n_op):
    cores = 2 if n_sector % 2 == 0 else 1
    ny = 1
    while ny * ny * 4 <= n_op and n_op % (ny * 2) == 0:
        ny *= 2
    return n_sector // cores, cores, n_op // ny, ny


class Place:
    def __init__(self, dims):
        self.dims = dims
        nx, nc, nz, ny = dims
        sector, op = lax.axis_index("sector"), lax.axis_index("op")
        self.x, self.c = sector // nc, sector % nc
        self.z, self.y = op // ny, op % ny

    def at(self, x=0, c=0, z=0, y=0):
        nx, nc, nz, ny = self.dims
        return (
            lax.rem(self.x + x, nx),
            lax.rem(self.c + c, nc),
            lax.rem(self.z + z, nz),
            lax.rem(self.y + y, ny),
        )

    def device(self, **shift):
        nx, nc, nz, ny = self.dims
        x, c, z, y = self.at(**shift)
        return (x * nc + c, z * ny + y)

    def greet(self):
        barrier = pltpu.get_barrier_semaphore()
        count = 0
        for name, n in zip("xczy", self.dims):
            for shift in range(1, n):
                pl.semaphore_signal(
                    barrier, inc=1, device_id=self.device(**{name: shift}), device_id_type=MESH
                )
                count += 1
        pl.semaphore_wait(barrier, count)


def remote(src, dst, send, recv, device):
    return pltpu.make_async_remote_copy(
        src_ref=src, dst_ref=dst, send_sem=send, recv_sem=recv, device_id=device, device_id_type=MESH
    )


def gather_kernel(
    dims, wave_ref, base_ref, wave_all, base_all,
    local, wzs, wzr, wys, wyr, bzs, bzr, bys, byr, bxs, bxr, bcs, bcr,
):
    nx, nc, nz, ny = dims
    me = Place(dims)
    per_owner, slab, _ = wave_ref.shape

    def rows(z, y):
        return pl.ds((z * ny + y) * slab, slab)

    def wave(d, e):
        _, _, z, y = me.at(z=nz - d, y=ny - e)
        return wave_all.at[:, rows(z, y), :]

    def base(d, e, f, g):
        x, c, z, y = me.at(x=nx - f, c=nc - g, z=nz - d, y=ny - e)
        return base_all.at[pl.ds((x * nc + c) * per_owner, per_owner), rows(z, y), :]

    keep_wave = pltpu.make_async_copy(wave_ref, wave(0, 0), local.at[0])
    keep_base = pltpu.make_async_copy(base_ref, base(0, 0, 0, 0), local.at[1])

    def wave_z(d):
        return remote(wave_ref, wave(0, 0), wzs.at[d], wzr.at[d], me.device(z=d))

    def wave_y(d, e, src):
        return remote(src, wave(d, 0), wys.at[e, d], wyr.at[e, d], me.device(y=e))

    def base_z(d):
        return remote(base_ref, base(0, 0, 0, 0), bzs.at[d], bzr.at[d], me.device(z=d))

    def base_y(d, e, src):
        return remote(src, base(d, 0, 0, 0), bys.at[e, d], byr.at[e, d], me.device(y=e))

    def base_x(d, e, f, src):
        return remote(src, base(d, e, 0, 0), bxs.at[f, e, d], bxr.at[f, e, d], me.device(x=f))

    def base_c(d, e, f, g, src):
        return remote(src, base(d, e, f, 0), bcs.at[f, e, d], bcr.at[f, e, d], me.device(c=g))

    me.greet()
    keep_wave.start()
    keep_base.start()
    for e in range(1, ny):
        wave_y(0, e, wave_ref).start()
    for d in range(1, nz):
        wave_z(d).start()
    for f in range(1, nx):
        base_x(0, 0, f, base_ref).start()
    for g in range(1, nc):
        base_c(0, 0, 0, g, base_ref).start()
    for e in range(1, ny):
        base_y(0, e, base_ref).start()
    for d in range(1, nz):
        base_z(d).start()
    for d in range(1, nz):
        wave_z(d).wait_recv()
        for e in range(1, ny):
            wave_y(d, e, wave(d, 0)).start()

    def forward_x(d, e):
        for f in range(1, nx):
            base_x(d, e, f, base(d, e, 0, 0)).start()
        for g in range(1, nc):
            base_c(d, e, 0, g, base(d, e, 0, 0)).start()

    for e in range(1, ny):
        base_y(0, e, base(0, 0, 0, 0)).wait_recv()
        forward_x(0, e)
    for d in range(1, nz):
        base_z(d).wait_recv()
        for e in range(1, ny):
            base_y(d, e, base(d, 0, 0, 0)).start()
        forward_x(d, 0)
    for e in range(1, ny):

        @pl.loop(1, nz)
        def _(d):
            base_y(d, e, base(d, 0, 0, 0)).wait_recv()
            forward_x(d, e)

    for f in range(1, nx):
        for e in range(ny):

            @pl.loop(0, nz)
            def _(d):
                base_x(d, e, f, base(d, e, 0, 0)).wait_recv()
                for g in range(1, nc):
                    base_c(d, e, f, g, base(d, e, f, 0)).start()

    keep_wave.wait()
    keep_base.wait()
    for d in range(1, nz):
        wave_z(d).wait_send()
        base_z(d).wait_send()
    for e in range(1, ny):

        @pl.loop(0, nz)
        def _(d):
            wave_y(d, e, wave(d, 0)).wait()
            base_y(d, e, base(d, 0, 0, 0)).wait_send()

    for e in range(ny):

        @pl.loop(0, nz)
        def _(d):
            for f in range(1, nx):
                base_x(d, e, f, base(d, e, 0, 0)).wait_send()
            for f in range(nx):
                for g in range(1, nc):
                    base_c(d, e, f, g, base(d, e, f, 0)).wait()


def gather(dims, wavefunction, sector_bases):
    nx, nc, nz, ny = dims
    per_owner, slab, width = wavefunction.shape
    dma = pltpu.SemaphoreType.DMA
    return pl.pallas_call(
        functools.partial(gather_kernel, dims),
        out_shape=(
            jax.ShapeDtypeStruct((per_owner, nz * ny * slab, width), wavefunction.dtype),
            jax.ShapeDtypeStruct((nx * nc * per_owner, nz * ny * slab, width), sector_bases.dtype),
        ),
        in_specs=[VMEM, VMEM],
        out_specs=(ANY, ANY),
        scratch_shapes=[dma((2,))]
        + [dma((nz,)), dma((nz,)), dma((ny, nz)), dma((ny, nz))] * 2
        + [dma((nx, ny, nz))] * 4,
        compiler_params=pltpu.CompilerParams(collective_id=0, has_side_effects=True),
        name="gather",
    )(wavefunction, sector_bases)


def order_of(slot, sector_slot, orders, sectors):
    total = jnp.int32(0)
    for i in range(sectors):
        total = total + jnp.where(sector_slot[i] == slot, orders[i], 0)
    return total


def pair_kernel(
    sectors, source, target, sector_slot, orders, wave, bases, left, right, sigma, rotated, masked, total
):
    step = pl.program_id(0)
    per_owner, width, _ = wave.shape
    first = lax.axis_index("sector") * per_owner

    @pl.when(step == 0)
    def _():
        total[...] = jnp.zeros_like(total)
        row = lax.broadcasted_iota(jnp.int32, (width, width), 0)
        column = lax.broadcasted_iota(jnp.int32, (width, width), 1)
        for j in range(per_owner):
            order = order_of(first + j, sector_slot, orders, sectors)
            inside = jnp.maximum(row, column) < order
            masked[j] = jnp.where(inside, wave[j], jnp.zeros((), wave.dtype))

    a = sector_slot[source[step]]
    b = sector_slot[target[step]]
    block = left[0]
    projected = jnp.dot(block, masked[a - first], preferred_element_type=jnp.float32)
    half = jnp.dot(block, bases[a], preferred_element_type=jnp.float32)
    total[b] += lax.dot_general(
        projected.astype(block.dtype), right[0], (((1,), (1,)), ((), ())),
        preferred_element_type=jnp.float32,
    )
    rotated[0] = lax.dot_general(
        bases[b], half.astype(block.dtype), (((0,), (0,)), ((), ())),
        preferred_element_type=jnp.float32,
    ).astype(rotated.dtype)

    @pl.when(step == pl.num_programs(0) - 1)
    def _():
        @pl.loop(0, total.shape[0])
        def _(q):
            sigma[q] = total[q].astype(sigma.dtype)


def pairs(wave, bases, left, right, source, target, sector_slot, orders):
    count, width, _ = left.shape
    sectors = sector_slot.shape[0]
    whole = lambda shape: pl.BlockSpec(
        shape, lambda p, *_: (0, 0, 0), pipeline_mode=pl.Buffered(1)
    )
    each = pl.BlockSpec((1, width, width), lambda p, *_: (p, 0, 0))
    return pl.pallas_call(
        functools.partial(pair_kernel, sectors),
        out_shape=(
            jax.ShapeDtypeStruct(bases.shape, jnp.bfloat16),
            jax.ShapeDtypeStruct(left.shape, left.dtype),
        ),
        grid_spec=pltpu.PrefetchScalarGridSpec(
            num_scalar_prefetch=4,
            grid=(count,),
            in_specs=[whole(wave.shape), whole(bases.shape), each, each],
            out_specs=(whole(bases.shape), each),
            scratch_shapes=[
                pltpu.VMEM(wave.shape, wave.dtype),
                pltpu.VMEM(bases.shape, jnp.float32),
            ],
        ),
        compiler_params=pltpu.CompilerParams(
            dimension_semantics=("arbitrary",), vmem_limit_bytes=60 * 1024 * 1024
        ),
        name="pairs",
    )(source, target, sector_slot, orders, wave, bases, left, right)


def reduce_kernel(
    dims, sectors, part, sector_slot, orders, out,
    got_c, send_1, got_1, mid, send_2, got_2, held, send_3, got_3,
    cs, cr, s1, r1, s2, r2, s3, r3,
):
    nx, nc, nz, ny = dims
    me = Place(dims)
    per_owner, slab, width = out.shape
    strip = ny * slab
    f32, bf16 = jnp.float32, jnp.bfloat16
    first = "xy"
    size = {"x": nx, "y": ny}

    def axes(j):
        return ("x", "y") if j % 2 == 0 else ("y", "x")

    def zq(d):
        return lax.rem(me.z + d, nz)

    def core_copy(x, j, d):
        slot = (x * nc + lax.rem(me.c + 1, nc)) * per_owner + j
        return remote(
            part.at[slot, pl.ds(zq(d) * strip, strip), :], got_c.at[d, j, x],
            cs.at[d, j, x], cr.at[d, j, x], me.device(c=1),
        )

    def copy_1(j, d, k):
        return remote(
            send_1.at[d, j, k], got_1.at[d, j, k], s1.at[d, j, k], r1.at[d, j, k],
            me.device(**{axes(j)[0]: k}),
        )

    def copy_2(j, d, k):
        return remote(
            send_2.at[d, j, k], got_2.at[d, j, k], s2.at[d, j, k], r2.at[d, j, k],
            me.device(**{axes(j)[1]: k}),
        )

    def copy_3(j, d):
        return remote(
            send_3.at[d, j], got_3.at[d, j], s3.at[d, j], r3.at[d, j], me.device(z=d)
        )

    def unit(d):
        return lax.rem(d + 1, nz)

    me.greet()
    if nc > 1:

        @pl.loop(0, nz)
        def _(i):
            for j in range(per_owner):
                for x in range(nx):
                    core_copy(x, j, unit(i)).start()

    @pl.loop(0, nz)
    def _(i):
        d = unit(i)
        for j in range(per_owner):
            n1 = size[axes(j)[0]]
            n2 = size[axes(j)[1]]

            def summed(x, row, count):
                slot = (x * nc + me.c) * per_owner + j
                value = part[slot, pl.ds(zq(d) * strip + row, count), :].astype(f32)
                if nc > 1:
                    value = value + got_c[d, j, x, pl.ds(row, count), :].astype(f32)
                return value

            if nc > 1:
                for x in range(nx):
                    core_copy(x, j, d).wait_recv()
            for k in list(range(1, n1)) + [0]:
                for m in range(n2):
                    if axes(j)[0] == "x":
                        x, y = lax.rem(me.x + k, nx), m
                    else:
                        x, y = m, lax.rem(me.y + k, ny)
                    value = summed(x, pl.multiple_of(y * slab, slab), slab)
                    if k:
                        send_1[d, j, k, m] = value.astype(bf16)
                    else:
                        mid[d, j, m] = value
                if k:
                    copy_1(j, d, k).start()

    @pl.loop(0, nz)
    def _(i):
        d = unit(i)
        for j in range(per_owner):
            axis_1, axis_2 = axes(j)
            n1, n2 = size[axis_1], size[axis_2]
            for k in range(1, n1):
                copy_1(j, d, k).wait_recv()
            for h in list(range(1, n2)) + [0]:
                m = lax.rem(getattr(me, axis_2) + h, n2)
                value = mid[d, j, m]
                for k in range(1, n1):
                    value = value + got_1[d, j, k, m].astype(f32)
                if h:
                    send_2[d, j, h] = value.astype(bf16)
                    copy_2(j, d, h).start()
                else:
                    held[d, j] = value

    def stage_3(d, j):
        for h in range(1, size[axes(j)[1]]):
            copy_2(j, d, h).wait_recv()
        value = held[d, j]
        for h in range(1, size[axes(j)[1]]):
            value = value + got_2[d, j, h].astype(f32)
        return value

    @pl.loop(1, nz)
    def _(d):
        for j in range(per_owner):
            send_3[d, j] = stage_3(d, j).astype(bf16)
            copy_3(j, d).start()

    own = (me.x * nc + me.c) * per_owner
    row = lax.broadcasted_iota(jnp.int32, (slab, width), 0) + (me.z * ny + me.y) * slab
    column = lax.broadcasted_iota(jnp.int32, (slab, width), 1)
    for j in range(per_owner):
        value = stage_3(0, j)
        for d in range(1, nz):
            copy_3(j, d).wait_recv()
            value = value + got_3[d, j].astype(f32)
        order = order_of(own + j, sector_slot, orders, sectors)
        inside = jnp.maximum(row, column) < order
        out[j] = jnp.where(inside, value, 0.0).astype(out.dtype)

    @pl.loop(0, nz)
    def _(d):
        for j in range(per_owner):
            if nc > 1:
                for x in range(nx):
                    core_copy(x, j, d).wait_send()
            for k in range(1, size[axes(j)[0]]):
                copy_1(j, d, k).wait_send()
            for h in range(1, size[axes(j)[1]]):
                copy_2(j, d, h).wait_send()

    @pl.loop(1, nz)
    def _(d):
        for j in range(per_owner):
            copy_3(j, d).wait_send()


def reduce(dims, part, sector_slot, orders, slab):
    nx, nc, nz, ny = dims
    sectors, _, width = part.shape
    per_owner = sectors // (nx * nc)
    most = max(nx, ny)
    dma = pltpu.SemaphoreType.DMA
    bf16, f32 = jnp.bfloat16, jnp.float32
    return pl.pallas_call(
        functools.partial(reduce_kernel, dims, sectors),
        out_shape=jax.ShapeDtypeStruct((per_owner, slab, width), bf16),
        in_specs=[VMEM, SMEM, SMEM],
        out_specs=VMEM,
        scratch_shapes=[
            pltpu.VMEM((nz, per_owner, nx, ny * slab, width), bf16),
            pltpu.VMEM((nz, per_owner, most, most, slab, width), bf16),
            pltpu.VMEM((nz, per_owner, most, most, slab, width), bf16),
            pltpu.VMEM((nz, per_owner, most, slab, width), f32),
            pltpu.VMEM((nz, per_owner, most, slab, width), bf16),
            pltpu.VMEM((nz, per_owner, most, slab, width), bf16),
            pltpu.VMEM((nz, per_owner, slab, width), f32),
            pltpu.VMEM((nz, per_owner, slab, width), bf16),
            pltpu.VMEM((nz, per_owner, slab, width), bf16),
        ]
        + [dma((nz, per_owner, nx))] * 2
        + [dma((nz, per_owner, most))] * 4
        + [dma((nz, per_owner))] * 2,
        compiler_params=pltpu.CompilerParams(
            collective_id=1, has_side_effects=True, vmem_limit_bytes=60 * 1024 * 1024
        ),
        name="reduce",
    )(part, sector_slot, orders)


def solution(mesh):
    dims = grid_of(mesh.shape["sector"], mesh.shape["op"])

    def per_device(
        wavefunction, sector_bases, left_env, right_env, pair_source, pair_target, sector_slot, orders
    ):
        wave, bases = gather(dims, wavefunction, sector_bases)
        part, left_rotated = pairs(
            wave, bases, left_env, right_env, pair_source, pair_target, sector_slot, orders
        )
        sigma_blocks = reduce(dims, part, sector_slot, orders, wavefunction.shape[1])
        return sigma_blocks, left_rotated

    placed = (
        P("sector", "op", None),
        P("sector", "op", None),
        P(("sector", "op"), None, None),
        P(("sector", "op"), None, None),
        P(("sector", "op")),
        P(("sector", "op")),
        P(),
        P(),
    )
    return jax.shard_map(
        per_device,
        mesh=mesh,
        in_specs=placed,
        out_specs=(P("sector", "op", None), P(("sector", "op"), None, None)),
        check_vma=False,
    )
```

```python
import functools

import jax
import jax.numpy as jnp
from jax import lax
from jax.experimental import pallas as pl
from jax.experimental.pallas import tpu as pltpu
from jax.sharding import PartitionSpec as P

MESH = pl.DeviceIdType.MESH
ANY = pl.BlockSpec(memory_space=pl.ANY)
VMEM = pl.BlockSpec(memory_space=pltpu.VMEM)
SMEM = pl.BlockSpec(memory_space=pltpu.SMEM)


def grid_of(n_sector, n_op):
    cores = 2 if n_sector % 2 == 0 else 1
    ny = 1
    while ny * ny * 4 <= n_op and n_op % (ny * 2) == 0:
        ny *= 2
    return n_sector // cores, cores, n_op // ny, ny


class Place:
    def __init__(self, dims):
        self.dims = dims
        nx, nc, nz, ny = dims
        sector, op = lax.axis_index("sector"), lax.axis_index("op")
        self.x, self.c = sector // nc, sector % nc
        self.z, self.y = op // ny, op % ny

    def at(self, x=0, c=0, z=0, y=0):
        nx, nc, nz, ny = self.dims
        return (
            lax.rem(self.x + x, nx),
            lax.rem(self.c + c, nc),
            lax.rem(self.z + z, nz),
            lax.rem(self.y + y, ny),
        )

    def device(self, **shift):
        nx, nc, nz, ny = self.dims
        x, c, z, y = self.at(**shift)
        return (x * nc + c, z * ny + y)

    def greet(self):
        barrier = pltpu.get_barrier_semaphore()
        count = 0
        for name, n in zip("xczy", self.dims):
            for shift in range(1, n):
                pl.semaphore_signal(
                    barrier, inc=1, device_id=self.device(**{name: shift}), device_id_type=MESH
                )
                count += 1
        pl.semaphore_wait(barrier, count)


def remote(src, dst, send, recv, device):
    return pltpu.make_async_remote_copy(
        src_ref=src, dst_ref=dst, send_sem=send, recv_sem=recv, device_id=device, device_id_type=MESH
    )


def order_of(slot, sector_slot, orders, sectors):
    total = jnp.int32(0)
    for i in range(sectors):
        total = total + jnp.where(sector_slot[i] == slot, orders[i], 0)
    return total


def sigma_kernel(
    dims, sectors, wave_ref, base_ref, left_hbm, right_hbm, source, target, sector_slot, orders,
    out, base_all,
    wave_all, masked, left, right, product,
    send_c, got_c, send_1, got_1, mid, send_2, got_2, held, send_3, got_3,
    local, wzs, wzr, bzs, bzr, wys, wyr, bys, byr, bxs, bxr, bcs, bcr,
    cs, cr, s1, r1, s2, r2, s3, r3,
):
    nx, nc, nz, ny = dims
    me = Place(dims)
    per_owner, slab, width = out.shape
    count = left.shape[0]
    strip = ny * slab
    f32, bf16 = jnp.float32, jnp.bfloat16
    size = {"x": nx, "y": ny}
    first = (me.x * nc + me.c) * per_owner

    def rows(z, y):
        return pl.ds((z * ny + y) * slab, slab)

    def wave(z, e=0):
        return wave_all.at[:, rows(z, lax.rem(me.y + ny - e, ny)), :]

    def base(z, e=0, f=0, g=0):
        x, c, _, y = me.at(x=nx - f, c=nc - g, y=ny - e)
        return base_all.at[pl.ds((x * nc + c) * per_owner, per_owner), rows(z, y), :]

    keep_wave = pltpu.make_async_copy(wave_ref, wave(me.z), local.at[0])
    keep_base = pltpu.make_async_copy(base_ref, base(me.z), local.at[1])
    take_left = pltpu.make_async_copy(left_hbm, left, local.at[2])
    take_right = pltpu.make_async_copy(right_hbm, right, local.at[3])

    def chain(block, send, recv, up, z, src):
        shift = 1 if up else nz - 1
        return remote(
            src, block(z), send.at[0 if up else 1, z], recv.at[z], me.device(z=shift)
        )

    def wave_z(up, z, src):
        return chain(wave, wzs, wzr, up, z, src)

    def base_z(up, z, src):
        return chain(base, bzs, bzr, up, z, src)

    def wave_y(z, e, src):
        return remote(src, wave(z), wys.at[e, z], wyr.at[e, z], me.device(y=e))

    def base_y(z, e, src):
        return remote(src, base(z), bys.at[e, z], byr.at[e, z], me.device(y=e))

    def base_x(z, e, f, src):
        return remote(src, base(z, e), bxs.at[f, e, z], bxr.at[f, e, z], me.device(x=f))

    def base_c(z, e, f, g, src):
        return remote(src, base(z, e, f), bcs.at[f, e, z], bcr.at[f, e, z], me.device(c=g))

    def each_far_z(visit):
        for d in range(1, nz):

            @pl.when(me.z >= d)
            def _():
                visit(me.z - d, True)

            @pl.when(me.z + d < nz)
            def _():
                visit(me.z + d, False)

    def both_ways(start, src):
        @pl.when(me.z < nz - 1)
        def _():
            start(True, me.z, src).start()

        @pl.when(me.z > 0)
        def _():
            start(False, me.z, src).start()

    def relay(copy, block, z, up):
        copy(up, z, block(z)).wait_recv()

        @pl.when(me.z < nz - 1 if up else me.z > 0)
        def _():
            copy(up, z, block(z)).start()

    def forward_x(z, e, src):
        for f in range(1, nx):
            base_x(z, e, f, src).start()
        for g in range(1, nc):
            base_c(z, e, 0, g, src).start()

    me.greet()
    both_ways(wave_z, wave_ref)
    for e in range(1, ny):
        wave_y(me.z, e, wave_ref).start()
    keep_wave.start()
    take_left.start()
    take_right.start()
    keep_base.start()
    both_ways(base_z, base_ref)
    forward_x(me.z, 0, base_ref)

    def on_wave(z, up):
        relay(wave_z, wave, z, up)
        for e in range(1, ny):
            wave_y(z, e, wave(z)).start()

    each_far_z(on_wave)
    for e in range(1, ny):
        base_y(me.z, e, base_ref).start()

    def on_base(z, up):
        relay(base_z, base, z, up)
        forward_x(z, 0, base(z))
        for e in range(1, ny):
            base_y(z, e, base(z)).start()

    each_far_z(on_base)
    keep_wave.wait()
    take_left.wait()
    take_right.wait()
    for e in range(1, ny):

        @pl.loop(0, nz)
        def _(z):
            wave_y(z, e, wave(z, e)).wait_recv()

    row = lax.broadcasted_iota(jnp.int32, (width, width), 0)
    column = lax.broadcasted_iota(jnp.int32, (width, width), 1)
    for j in range(per_owner):
        order = order_of(first + j, sector_slot, orders, sectors)
        inside = jnp.maximum(row, column) < order
        masked[j] = jnp.where(inside, wave_all[j], jnp.zeros((), bf16))

    @pl.loop(0, count)
    def _(p):
        a = lax.rem(sector_slot[source[p]], per_owner)
        projected = jnp.dot(left[p], masked[a], preferred_element_type=f32)
        product[p] = lax.dot_general(
            projected.astype(bf16), right[p], (((1,), (1,)), ((), ())),
            preferred_element_type=f32,
        )

    landed = [sector_slot[target[p]] for p in range(count)]

    def partial_sum(slot, start, size):
        total = None
        for p in range(count):
            weight = jnp.where(landed[p] == slot, 1.0, 0.0).astype(f32)
            term = product[p, pl.ds(start, size), :] * weight
            total = term if total is None else total + term
        return total

    def axes(j):
        return ("x", "y") if j % 2 == 0 else ("y", "x")

    def zq(d):
        return lax.rem(me.z + d, nz)

    def core_copy(x, j, d):
        return remote(
            send_c.at[d, j, x], got_c.at[d, j, x], cs.at[d, j, x], cr.at[d, j, x], me.device(c=1)
        )

    def copy_1(j, d, k):
        return remote(
            send_1.at[d, j, k], got_1.at[d, j, k], s1.at[d, j, k], r1.at[d, j, k],
            me.device(**{axes(j)[0]: k}),
        )

    def copy_2(j, d, k):
        return remote(
            send_2.at[d, j, k], got_2.at[d, j, k], s2.at[d, j, k], r2.at[d, j, k],
            me.device(**{axes(j)[1]: k}),
        )

    def copy_3(j, d):
        return remote(
            send_3.at[d, j], got_3.at[d, j], s3.at[d, j], r3.at[d, j], me.device(z=d)
        )

    def unit(d):
        return lax.rem(d + 1, nz)

    if nc > 1:

        @pl.loop(0, nz)
        def _(i):
            d = unit(i)
            for j in range(per_owner):
                for x in range(nx):
                    slot = (x * nc + lax.rem(me.c + 1, nc)) * per_owner + j
                    for m in range(ny):
                        value = partial_sum(slot, pl.multiple_of(zq(d) * strip + m * slab, slab), slab)
                        send_c[d, j, x, pl.ds(m * slab, slab), :] = value.astype(bf16)
                    core_copy(x, j, d).start()

    @pl.loop(0, nz)
    def _(i):
        d = unit(i)
        for j in range(per_owner):
            n1 = size[axes(j)[0]]
            n2 = size[axes(j)[1]]
            if nc > 1:
                for x in range(nx):
                    core_copy(x, j, d).wait_recv()
            for k in list(range(1, n1)) + [0]:
                for m in range(n2):
                    if axes(j)[0] == "x":
                        x, y = lax.rem(me.x + k, nx), m
                    else:
                        x, y = m, lax.rem(me.y + k, ny)
                    offset = pl.multiple_of(y * slab, slab)
                    slot = (x * nc + me.c) * per_owner + j
                    value = partial_sum(slot, pl.multiple_of(zq(d) * strip + offset, slab), slab)
                    if nc > 1:
                        value = value + got_c[d, j, x, pl.ds(offset, slab), :].astype(f32)
                    if k:
                        send_1[d, j, k, m] = value.astype(bf16)
                    else:
                        mid[d, j, m] = value
                if k:
                    copy_1(j, d, k).start()

    for e in range(1, ny):

        @pl.loop(0, nz)
        def _(i):
            z = lax.rem(me.z + i, nz)
            base_y(z, e, base(z, e)).wait_recv()
            forward_x(z, e, base(z, e))

    @pl.loop(0, nz)
    def _(i):
        d = unit(i)
        for j in range(per_owner):
            axis_1, axis_2 = axes(j)
            n1, n2 = size[axis_1], size[axis_2]
            for k in range(1, n1):
                copy_1(j, d, k).wait_recv()
            for h in list(range(1, n2)) + [0]:
                m = lax.rem(getattr(me, axis_2) + h, n2)
                value = mid[d, j, m]
                for k in range(1, n1):
                    value = value + got_1[d, j, k, m].astype(f32)
                if h:
                    send_2[d, j, h] = value.astype(bf16)
                    copy_2(j, d, h).start()
                else:
                    held[d, j] = value

    for f in range(1, nx):
        for e in range(1):

            @pl.loop(0, nz)
            def _(z):
                base_x(z, e, f, base(z, e, f)).wait_recv()
                for g in range(1, nc):
                    base_c(z, e, f, g, base(z, e, f)).start()

    def stage_3(d, j):
        for h in range(1, size[axes(j)[1]]):
            copy_2(j, d, h).wait_recv()
        value = held[d, j]
        for h in range(1, size[axes(j)[1]]):
            value = value + got_2[d, j, h].astype(f32)
        return value

    @pl.loop(1, nz)
    def _(d):
        for j in range(per_owner):
            send_3[d, j] = stage_3(d, j).astype(bf16)
            copy_3(j, d).start()

    for f in range(1, nx):
        for e in range(1, ny):

            @pl.loop(0, nz)
            def _(i):
                z = lax.rem(me.z + i, nz)
                base_x(z, e, f, base(z, e, f)).wait_recv()
                for g in range(1, nc):
                    base_c(z, e, f, g, base(z, e, f)).start()

    row = lax.broadcasted_iota(jnp.int32, (slab, width), 0) + (me.z * ny + me.y) * slab
    column = lax.broadcasted_iota(jnp.int32, (slab, width), 1)
    for j in range(per_owner):
        value = stage_3(0, j)
        for d in range(1, nz):
            copy_3(j, d).wait_recv()
            value = value + got_3[d, j].astype(f32)
        order = order_of(first + j, sector_slot, orders, sectors)
        inside = jnp.maximum(row, column) < order
        out[j] = jnp.where(inside, value, 0.0).astype(out.dtype)

    keep_base.wait()
    for start, block in ((wave_z, wave), (base_z, base)):

        @pl.when(me.z < nz - 1)
        def _():
            @pl.loop(0, me.z + 1)
            def _(z):
                start(True, z, block(z)).wait_send()

        @pl.when(me.z > 0)
        def _():
            @pl.loop(me.z, nz)
            def _(z):
                start(False, z, block(z)).wait_send()

    @pl.loop(0, nz)
    def _(z):
        for e in range(1, ny):
            wave_y(z, e, wave(z)).wait_send()
            base_y(z, e, base(z)).wait_send()
        for e in range(ny):
            for f in range(1, nx):
                base_x(z, e, f, base(z, e)).wait_send()
            for f in range(nx):
                for g in range(1, nc):
                    base_c(z, e, f, g, base(z, e, f)).wait()

    @pl.loop(0, nz)
    def _(d):
        for j in range(per_owner):
            if nc > 1:
                for x in range(nx):
                    core_copy(x, j, d).wait_send()
            for k in range(1, size[axes(j)[0]]):
                copy_1(j, d, k).wait_send()
            for h in range(1, size[axes(j)[1]]):
                copy_2(j, d, h).wait_send()

    @pl.loop(1, nz)
    def _(d):
        for j in range(per_owner):
            copy_3(j, d).wait_send()


def sigma_and_bases(
    dims, wavefunction, sector_bases, left, right, source, target, sector_slot, orders
):
    nx, nc, nz, ny = dims
    per_owner, slab, width = wavefunction.shape
    sectors = sector_slot.shape[0]
    most = max(nx, ny)
    dma = pltpu.SemaphoreType.DMA
    bf16, f32 = jnp.bfloat16, jnp.float32
    full = (per_owner, nz * ny * slab, width)
    return pl.pallas_call(
        functools.partial(sigma_kernel, dims, sectors),
        out_shape=(
            jax.ShapeDtypeStruct((per_owner, slab, width), bf16),
            jax.ShapeDtypeStruct((sectors, nz * ny * slab, width), sector_bases.dtype),
        ),
        in_specs=[VMEM, VMEM, ANY, ANY, SMEM, SMEM, SMEM, SMEM],
        out_specs=(VMEM, ANY),
        scratch_shapes=[
            pltpu.VMEM(full, bf16),
            pltpu.VMEM(full, bf16),
            pltpu.VMEM(left.shape, bf16),
            pltpu.VMEM(right.shape, bf16),
            pltpu.VMEM(left.shape, f32),
            pltpu.VMEM((nz, per_owner, nx, ny * slab, width), bf16),
            pltpu.VMEM((nz, per_owner, nx, ny * slab, width), bf16),
            pltpu.VMEM((nz, per_owner, most, most, slab, width), bf16),
            pltpu.VMEM((nz, per_owner, most, most, slab, width), bf16),
            pltpu.VMEM((nz, per_owner, most, slab, width), f32),
            pltpu.VMEM((nz, per_owner, most, slab, width), bf16),
            pltpu.VMEM((nz, per_owner, most, slab, width), bf16),
            pltpu.VMEM((nz, per_owner, slab, width), f32),
            pltpu.VMEM((nz, per_owner, slab, width), bf16),
            pltpu.VMEM((nz, per_owner, slab, width), bf16),
        ]
        + [dma((4,))]
        + [dma((2, nz)), dma((nz,))] * 2
        + [dma((ny, nz))] * 4
        + [dma((nx, ny, nz))] * 4
        + [dma((nz, per_owner, nx))] * 2
        + [dma((nz, per_owner, most))] * 4
        + [dma((nz, per_owner))] * 2,
        compiler_params=pltpu.CompilerParams(
            collective_id=0, has_side_effects=True, vmem_limit_bytes=60 * 1024 * 1024
        ),
        name="sigma",
    )(wavefunction, sector_bases, left, right, source, target, sector_slot, orders)


def rotate_kernel(source, target, sector_slot, bases, left, rotated):
    step = pl.program_id(0)
    a = sector_slot[source[step]]
    b = sector_slot[target[step]]
    half = jnp.dot(left[0], bases[a], preferred_element_type=jnp.float32)
    rotated[0] = lax.dot_general(
        bases[b], half.astype(bases.dtype), (((0,), (0,)), ((), ())),
        preferred_element_type=jnp.float32,
    ).astype(rotated.dtype)


def rotate(bases, left, source, target, sector_slot):
    count, width, _ = left.shape
    each = pl.BlockSpec((1, width, width), lambda p, *_: (p, 0, 0))
    return pl.pallas_call(
        rotate_kernel,
        out_shape=jax.ShapeDtypeStruct(left.shape, left.dtype),
        grid_spec=pltpu.PrefetchScalarGridSpec(
            num_scalar_prefetch=3,
            grid=(count,),
            in_specs=[
                pl.BlockSpec(bases.shape, lambda p, *_: (0, 0, 0), pipeline_mode=pl.Buffered(1)),
                each,
            ],
            out_specs=each,
        ),
        compiler_params=pltpu.CompilerParams(
            dimension_semantics=("arbitrary",), vmem_limit_bytes=60 * 1024 * 1024
        ),
        name="rotate",
    )(source, target, sector_slot, bases, left)


def solution(mesh):
    dims = grid_of(mesh.shape["sector"], mesh.shape["op"])

    def per_device(
        wavefunction, sector_bases, left_env, right_env, pair_source, pair_target, sector_slot, orders
    ):
        sigma_blocks, bases = sigma_and_bases(
            dims, wavefunction, sector_bases, left_env, right_env,
            pair_source, pair_target, sector_slot, orders,
        )
        left_rotated = rotate(bases, left_env, pair_source, pair_target, sector_slot)
        return sigma_blocks, left_rotated

    placed = (
        P("sector", "op", None),
        P("sector", "op", None),
        P(("sector", "op"), None, None),
        P(("sector", "op"), None, None),
        P(("sector", "op")),
        P(("sector", "op")),
        P(),
        P(),
    )
    return jax.shard_map(
        per_device,
        mesh=mesh,
        in_specs=placed,
        out_specs=(P("sector", "op", None), P(("sector", "op"), None, None)),
        check_vma=False,
    )
```

```python
import functools

import jax
import jax.numpy as jnp
from jax import lax
from jax.experimental import pallas as pl
from jax.experimental.pallas import tpu as pltpu
from jax.sharding import PartitionSpec as P

MESH = pl.DeviceIdType.MESH
ANY = pl.BlockSpec(memory_space=pl.ANY)
VMEM = pl.BlockSpec(memory_space=pltpu.VMEM)
SMEM = pl.BlockSpec(memory_space=pltpu.SMEM)


def grid_of(n_sector, n_op):
    cores = 2 if n_sector % 2 == 0 else 1
    ny = 1
    while ny * ny * 4 <= n_op and n_op % (ny * 2) == 0:
        ny *= 2
    return n_sector // cores, cores, n_op // ny, ny


class Place:
    def __init__(self, dims):
        self.dims = dims
        nx, nc, nz, ny = dims
        sector, op = lax.axis_index("sector"), lax.axis_index("op")
        self.x, self.c = sector // nc, sector % nc
        self.z, self.y = op // ny, op % ny

    def at(self, x=0, c=0, z=0, y=0):
        nx, nc, nz, ny = self.dims
        return (
            lax.rem(self.x + x, nx),
            lax.rem(self.c + c, nc),
            lax.rem(self.z + z, nz),
            lax.rem(self.y + y, ny),
        )

    def device(self, **shift):
        nx, nc, nz, ny = self.dims
        x, c, z, y = self.at(**shift)
        return (x * nc + c, z * ny + y)

    def greet(self):
        barrier = pltpu.get_barrier_semaphore()
        count = 0
        for name, n in zip("xczy", self.dims):
            for shift in range(1, n):
                pl.semaphore_signal(
                    barrier, inc=1, device_id=self.device(**{name: shift}), device_id_type=MESH
                )
                count += 1
        pl.semaphore_wait(barrier, count)


def remote(src, dst, send, recv, device):
    return pltpu.make_async_remote_copy(
        src_ref=src, dst_ref=dst, send_sem=send, recv_sem=recv, device_id=device, device_id_type=MESH
    )


def order_of(slot, sector_slot, orders, sectors):
    total = jnp.int32(0)
    for i in range(sectors):
        total = total + jnp.where(sector_slot[i] == slot, orders[i], 0)
    return total


def sigma_kernel(
    dims, sectors, wave_ref, base_ref, left_hbm, right_hbm, source, target, sector_slot, orders,
    out, base_all, half_out,
    wave_all, masked, own_bases, half, left, right, product,
    send_c, got_c, send_1, got_1, mid, send_2, got_2, held, send_3, got_3,
    local, wzs, wzr, bzs, bzr, wys, wyr, bys, byr, bxs, bxr, bcs, bcr,
    cs, cr, s1, r1, s2, r2, s3, r3,
):
    nx, nc, nz, ny = dims
    me = Place(dims)
    per_owner, slab, width = out.shape
    count = left.shape[0]
    strip = ny * slab
    f32, bf16 = jnp.float32, jnp.bfloat16
    size = {"x": nx, "y": ny}
    first = (me.x * nc + me.c) * per_owner

    def rows(z, y):
        return pl.ds((z * ny + y) * slab, slab)

    def wave(z, e=0):
        return wave_all.at[:, rows(z, lax.rem(me.y + ny - e, ny)), :]

    def base(z, e=0, f=0, g=0):
        x, c, _, y = me.at(x=nx - f, c=nc - g, y=ny - e)
        return base_all.at[pl.ds((x * nc + c) * per_owner, per_owner), rows(z, y), :]

    keep_wave = pltpu.make_async_copy(wave_ref, wave(me.z), local.at[0])
    keep_base = pltpu.make_async_copy(base_ref, base(me.z), local.at[1])
    take_left = pltpu.make_async_copy(left_hbm, left, local.at[2])
    take_right = pltpu.make_async_copy(right_hbm, right, local.at[3])

    def chain(block, send, recv, up, z, src):
        shift = 1 if up else nz - 1
        return remote(
            src, block(z), send.at[0 if up else 1, z], recv.at[z], me.device(z=shift)
        )

    def wave_z(up, z, src):
        return chain(wave, wzs, wzr, up, z, src)

    def base_z(up, z, src):
        return chain(base, bzs, bzr, up, z, src)

    def wave_y(z, e, src):
        return remote(src, wave(z), wys.at[e, z], wyr.at[e, z], me.device(y=e))

    def base_y(z, e, src):
        return remote(src, base(z), bys.at[e, z], byr.at[e, z], me.device(y=e))

    def base_x(z, e, f, src):
        return remote(src, base(z, e), bxs.at[f, e, z], bxr.at[f, e, z], me.device(x=f))

    def base_c(z, e, f, g, src):
        return remote(src, base(z, e, f), bcs.at[f, e, z], bcr.at[f, e, z], me.device(c=g))

    def each_far_z(visit):
        for d in range(1, nz):

            @pl.when(me.z >= d)
            def _():
                visit(me.z - d, True)

            @pl.when(me.z + d < nz)
            def _():
                visit(me.z + d, False)

    def both_ways(start, src):
        @pl.when(me.z < nz - 1)
        def _():
            start(True, me.z, src).start()

        @pl.when(me.z > 0)
        def _():
            start(False, me.z, src).start()

    def relay(copy, block, z, up):
        copy(up, z, block(z)).wait_recv()

        @pl.when(me.z < nz - 1 if up else me.z > 0)
        def _():
            copy(up, z, block(z)).start()

    def forward_x(z, e, src):
        for f in range(1, nx):
            base_x(z, e, f, src).start()
        for g in range(1, nc):
            base_c(z, e, 0, g, src).start()

    me.greet()
    both_ways(wave_z, wave_ref)
    for e in range(1, ny):
        wave_y(me.z, e, wave_ref).start()
    keep_wave.start()
    take_left.start()
    take_right.start()
    keep_base.start()
    both_ways(base_z, base_ref)
    forward_x(me.z, 0, base_ref)

    def on_wave(z, up):
        relay(wave_z, wave, z, up)
        for e in range(1, ny):
            wave_y(z, e, wave(z)).start()

    each_far_z(on_wave)
    for e in range(1, ny):
        base_y(me.z, e, base_ref).start()

    def on_base(z, up):
        relay(base_z, base, z, up)
        forward_x(z, 0, base(z))
        for e in range(1, ny):
            base_y(z, e, base(z)).start()

    each_far_z(on_base)
    keep_wave.wait()
    take_left.wait()
    take_right.wait()
    for e in range(1, ny):

        @pl.loop(0, nz)
        def _(z):
            wave_y(z, e, wave(z, e)).wait_recv()

    row = lax.broadcasted_iota(jnp.int32, (width, width), 0)
    column = lax.broadcasted_iota(jnp.int32, (width, width), 1)
    for j in range(per_owner):
        order = order_of(first + j, sector_slot, orders, sectors)
        inside = jnp.maximum(row, column) < order
        masked[j] = jnp.where(inside, wave_all[j], jnp.zeros((), bf16))

    early = min(count // 2, nz)

    def pass_on(i):
        z = lax.rem(me.z + i, nz)
        for e in range(1, ny):
            base_y(z, e, base(z, e)).wait_recv()
            forward_x(z, e, base(z, e))

    @pl.loop(0, count)
    def _(p):
        a = lax.rem(sector_slot[source[p]], per_owner)
        projected = jnp.dot(left[p], masked[a], preferred_element_type=f32)
        product[p] = lax.dot_general(
            projected.astype(bf16), right[p], (((1,), (1,)), ((), ())),
            preferred_element_type=f32,
        )

        @pl.when((lax.rem(p, 2) == 1) & (p < 2 * early))
        def _():
            pass_on(p // 2)

    landed = [sector_slot[target[p]] for p in range(count)]

    def partial_sum(slot, start, size):
        total = None
        for p in range(count):
            weight = jnp.where(landed[p] == slot, 1.0, 0.0).astype(f32)
            term = product[p, pl.ds(start, size), :] * weight
            total = term if total is None else total + term
        return total

    def axes(j):
        return ("x", "y") if j % 2 == 0 else ("y", "x")

    def zq(d):
        return lax.rem(me.z + d, nz)

    def core_copy(x, j, d):
        return remote(
            send_c.at[d, j, x], got_c.at[d, j, x], cs.at[d, j, x], cr.at[d, j, x], me.device(c=1)
        )

    def copy_1(j, d, k):
        return remote(
            send_1.at[d, j, k], got_1.at[d, j, k], s1.at[d, j, k], r1.at[d, j, k],
            me.device(**{axes(j)[0]: k}),
        )

    def copy_2(j, d, k):
        return remote(
            send_2.at[d, j, k], got_2.at[d, j, k], s2.at[d, j, k], r2.at[d, j, k],
            me.device(**{axes(j)[1]: k}),
        )

    def copy_3(j, d):
        return remote(
            send_3.at[d, j], got_3.at[d, j], s3.at[d, j], r3.at[d, j], me.device(z=d)
        )

    def unit(d):
        return lax.rem(d + 1, nz)

    if nc > 1:

        @pl.loop(0, nz)
        def _(i):
            d = unit(i)
            for j in range(per_owner):
                for x in range(nx):
                    slot = (x * nc + lax.rem(me.c + 1, nc)) * per_owner + j
                    for m in range(ny):
                        value = partial_sum(slot, pl.multiple_of(zq(d) * strip + m * slab, slab), slab)
                        send_c[d, j, x, pl.ds(m * slab, slab), :] = value.astype(bf16)
                    core_copy(x, j, d).start()

    @pl.loop(0, nz)
    def _(i):
        d = unit(i)
        for j in range(per_owner):
            n1 = size[axes(j)[0]]
            n2 = size[axes(j)[1]]
            if nc > 1:
                for x in range(nx):
                    core_copy(x, j, d).wait_recv()
            for k in list(range(1, n1)) + [0]:
                for m in range(n2):
                    if axes(j)[0] == "x":
                        x, y = lax.rem(me.x + k, nx), m
                    else:
                        x, y = m, lax.rem(me.y + k, ny)
                    offset = pl.multiple_of(y * slab, slab)
                    slot = (x * nc + me.c) * per_owner + j
                    value = partial_sum(slot, pl.multiple_of(zq(d) * strip + offset, slab), slab)
                    if nc > 1:
                        value = value + got_c[d, j, x, pl.ds(offset, slab), :].astype(f32)
                    if k:
                        send_1[d, j, k, m] = value.astype(bf16)
                    else:
                        mid[d, j, m] = value
                if k:
                    copy_1(j, d, k).start()

    @pl.loop(early, nz)
    def _(i):
        pass_on(i)

    keep_base.wait()
    take_bases = pltpu.make_async_copy(
        base_all.at[pl.ds(first, per_owner)], own_bases, local.at[4]
    )
    take_bases.start()
    take_bases.wait()

    @pl.loop(0, count)
    def _(p):
        a = lax.rem(sector_slot[source[p]], per_owner)
        half[p] = jnp.dot(left[p], own_bases[a], preferred_element_type=f32).astype(bf16)

    give_half = pltpu.make_async_copy(half, half_out, local.at[5])
    give_half.start()

    @pl.loop(0, nz)
    def _(i):
        d = unit(i)
        for j in range(per_owner):
            axis_1, axis_2 = axes(j)
            n1, n2 = size[axis_1], size[axis_2]
            for k in range(1, n1):
                copy_1(j, d, k).wait_recv()
            for h in list(range(1, n2)) + [0]:
                m = lax.rem(getattr(me, axis_2) + h, n2)
                value = mid[d, j, m]
                for k in range(1, n1):
                    value = value + got_1[d, j, k, m].astype(f32)
                if h:
                    send_2[d, j, h] = value.astype(bf16)
                    copy_2(j, d, h).start()
                else:
                    held[d, j] = value

    for f in range(1, nx):
        for e in range(1):

            @pl.loop(0, nz)
            def _(z):
                base_x(z, e, f, base(z, e, f)).wait_recv()
                for g in range(1, nc):
                    base_c(z, e, f, g, base(z, e, f)).start()

    def stage_3(d, j):
        for h in range(1, size[axes(j)[1]]):
            copy_2(j, d, h).wait_recv()
        value = held[d, j]
        for h in range(1, size[axes(j)[1]]):
            value = value + got_2[d, j, h].astype(f32)
        return value

    @pl.loop(1, nz)
    def _(d):
        for j in range(per_owner):
            send_3[d, j] = stage_3(d, j).astype(bf16)
            copy_3(j, d).start()

    for f in range(1, nx):
        for e in range(1, ny):

            @pl.loop(0, nz)
            def _(i):
                z = lax.rem(me.z + i, nz)
                base_x(z, e, f, base(z, e, f)).wait_recv()
                for g in range(1, nc):
                    base_c(z, e, f, g, base(z, e, f)).start()

    row = lax.broadcasted_iota(jnp.int32, (slab, width), 0) + (me.z * ny + me.y) * slab
    column = lax.broadcasted_iota(jnp.int32, (slab, width), 1)
    for j in range(per_owner):
        value = stage_3(0, j)
        for d in range(1, nz):
            copy_3(j, d).wait_recv()
            value = value + got_3[d, j].astype(f32)
        order = order_of(first + j, sector_slot, orders, sectors)
        inside = jnp.maximum(row, column) < order
        out[j] = jnp.where(inside, value, 0.0).astype(out.dtype)

    give_half.wait()
    for start, block in ((wave_z, wave), (base_z, base)):

        @pl.when(me.z < nz - 1)
        def _():
            @pl.loop(0, me.z + 1)
            def _(z):
                start(True, z, block(z)).wait_send()

        @pl.when(me.z > 0)
        def _():
            @pl.loop(me.z, nz)
            def _(z):
                start(False, z, block(z)).wait_send()

    @pl.loop(0, nz)
    def _(z):
        for e in range(1, ny):
            wave_y(z, e, wave(z)).wait_send()
            base_y(z, e, base(z)).wait_send()
        for e in range(ny):
            for f in range(1, nx):
                base_x(z, e, f, base(z, e)).wait_send()
            for f in range(nx):
                for g in range(1, nc):
                    base_c(z, e, f, g, base(z, e, f)).wait()

    @pl.loop(0, nz)
    def _(d):
        for j in range(per_owner):
            if nc > 1:
                for x in range(nx):
                    core_copy(x, j, d).wait_send()
            for k in range(1, size[axes(j)[0]]):
                copy_1(j, d, k).wait_send()
            for h in range(1, size[axes(j)[1]]):
                copy_2(j, d, h).wait_send()

    @pl.loop(1, nz)
    def _(d):
        for j in range(per_owner):
            copy_3(j, d).wait_send()


def sigma_and_bases(
    dims, wavefunction, sector_bases, left, right, source, target, sector_slot, orders
):
    nx, nc, nz, ny = dims
    per_owner, slab, width = wavefunction.shape
    sectors = sector_slot.shape[0]
    most = max(nx, ny)
    dma = pltpu.SemaphoreType.DMA
    bf16, f32 = jnp.bfloat16, jnp.float32
    full = (per_owner, nz * ny * slab, width)
    return pl.pallas_call(
        functools.partial(sigma_kernel, dims, sectors),
        out_shape=(
            jax.ShapeDtypeStruct((per_owner, slab, width), bf16),
            jax.ShapeDtypeStruct((sectors, nz * ny * slab, width), sector_bases.dtype),
            jax.ShapeDtypeStruct(left.shape, bf16),
        ),
        in_specs=[VMEM, VMEM, ANY, ANY, SMEM, SMEM, SMEM, SMEM],
        out_specs=(VMEM, ANY, ANY),
        scratch_shapes=[
            pltpu.VMEM(full, bf16),
            pltpu.VMEM(full, bf16),
            pltpu.VMEM(full, bf16),
            pltpu.VMEM(left.shape, bf16),
            pltpu.VMEM(left.shape, bf16),
            pltpu.VMEM(right.shape, bf16),
            pltpu.VMEM(left.shape, f32),
            pltpu.VMEM((nz, per_owner, nx, ny * slab, width), bf16),
            pltpu.VMEM((nz, per_owner, nx, ny * slab, width), bf16),
            pltpu.VMEM((nz, per_owner, most, most, slab, width), bf16),
            pltpu.VMEM((nz, per_owner, most, most, slab, width), bf16),
            pltpu.VMEM((nz, per_owner, most, slab, width), f32),
            pltpu.VMEM((nz, per_owner, most, slab, width), bf16),
            pltpu.VMEM((nz, per_owner, most, slab, width), bf16),
            pltpu.VMEM((nz, per_owner, slab, width), f32),
            pltpu.VMEM((nz, per_owner, slab, width), bf16),
            pltpu.VMEM((nz, per_owner, slab, width), bf16),
        ]
        + [dma((6,))]
        + [dma((2, nz)), dma((nz,))] * 2
        + [dma((ny, nz))] * 4
        + [dma((nx, ny, nz))] * 4
        + [dma((nz, per_owner, nx))] * 2
        + [dma((nz, per_owner, most))] * 4
        + [dma((nz, per_owner))] * 2,
        compiler_params=pltpu.CompilerParams(
            collective_id=0, has_side_effects=True, vmem_limit_bytes=60 * 1024 * 1024
        ),
        name="sigma",
    )(wavefunction, sector_bases, left, right, source, target, sector_slot, orders)


def rotate_kernel(target, sector_slot, basis, half, rotated):
    rotated[0] = lax.dot_general(
        basis[0], half[0], (((0,), (0,)), ((), ())), preferred_element_type=jnp.float32
    ).astype(rotated.dtype)


def rotate(bases, half, target, sector_slot):
    count, width, _ = half.shape
    each = pl.BlockSpec((1, width, width), lambda p, *_: (p, 0, 0))
    chosen = pl.BlockSpec((1, width, width), lambda p, target, slot: (slot[target[p]], 0, 0))
    return pl.pallas_call(
        rotate_kernel,
        out_shape=jax.ShapeDtypeStruct(half.shape, half.dtype),
        grid_spec=pltpu.PrefetchScalarGridSpec(
            num_scalar_prefetch=2, grid=(count,), in_specs=[chosen, each], out_specs=each
        ),
        compiler_params=pltpu.CompilerParams(
            dimension_semantics=("arbitrary",), vmem_limit_bytes=60 * 1024 * 1024
        ),
        name="rotate",
    )(target, sector_slot, bases, half)


def solution(mesh):
    dims = grid_of(mesh.shape["sector"], mesh.shape["op"])

    def per_device(
        wavefunction, sector_bases, left_env, right_env, pair_source, pair_target, sector_slot, orders
    ):
        sigma_blocks, bases, half = sigma_and_bases(
            dims, wavefunction, sector_bases, left_env, right_env,
            pair_source, pair_target, sector_slot, orders,
        )
        left_rotated = rotate(bases, half, pair_target, sector_slot)
        return sigma_blocks, left_rotated

    placed = (
        P("sector", "op", None),
        P("sector", "op", None),
        P(("sector", "op"), None, None),
        P(("sector", "op"), None, None),
        P(("sector", "op")),
        P(("sector", "op")),
        P(),
        P(),
    )
    return jax.shard_map(
        per_device,
        mesh=mesh,
        in_specs=placed,
        out_specs=(P("sector", "op", None), P(("sector", "op"), None, None)),
        check_vma=False,
    )
```

```python
import functools

import jax
import jax.numpy as jnp
from jax import lax
from jax.experimental import pallas as pl
from jax.experimental.pallas import tpu as pltpu
from jax.sharding import PartitionSpec as P

MESH = pl.DeviceIdType.MESH
ANY = pl.BlockSpec(memory_space=pl.ANY)
VMEM = pl.BlockSpec(memory_space=pltpu.VMEM)
SMEM = pl.BlockSpec(memory_space=pltpu.SMEM)


def grid_of(n_sector, n_op):
    cores = 2 if n_sector % 2 == 0 else 1
    ny = 1
    while ny * ny * 4 <= n_op and n_op % (ny * 2) == 0:
        ny *= 2
    return n_sector // cores, cores, n_op // ny, ny


class Place:
    def __init__(self, dims):
        self.dims = dims
        nx, nc, nz, ny = dims
        sector, op = lax.axis_index("sector"), lax.axis_index("op")
        self.x, self.c = sector // nc, sector % nc
        self.z, self.y = op // ny, op % ny

    def at(self, x=0, c=0, z=0, y=0):
        nx, nc, nz, ny = self.dims
        return (
            lax.rem(self.x + x, nx),
            lax.rem(self.c + c, nc),
            lax.rem(self.z + z, nz),
            lax.rem(self.y + y, ny),
        )

    def device(self, **shift):
        nx, nc, nz, ny = self.dims
        x, c, z, y = self.at(**shift)
        return (x * nc + c, z * ny + y)

    def greet(self):
        barrier = pltpu.get_barrier_semaphore()
        count = 0
        for name, n in zip("xczy", self.dims):
            for shift in range(1, n):
                pl.semaphore_signal(
                    barrier, inc=1, device_id=self.device(**{name: shift}), device_id_type=MESH
                )
                count += 1
        pl.semaphore_wait(barrier, count)


def remote(src, dst, send, recv, device):
    return pltpu.make_async_remote_copy(
        src_ref=src, dst_ref=dst, send_sem=send, recv_sem=recv, device_id=device, device_id_type=MESH
    )


def order_of(slot, sector_slot, orders, sectors):
    total = jnp.int32(0)
    for i in range(sectors):
        total = total + jnp.where(sector_slot[i] == slot, orders[i], 0)
    return total


def sigma_kernel(
    dims, sectors, wave_ref, base_ref, left_hbm, right_hbm, source, target, sector_slot, orders,
    out, base_all, half_out,
    wave_all, masked, own_bases, half, left, right, product,
    send_c, got_c, send_1, got_1, mid, send_2, got_2, held, send_3, got_3,
    local, hys, hyr, hzs, hzr, wzs, wzr, bzs, bzr, wys, wyr, bys, byr, bxs, bxr, bcs, bcr,
    cs, cr, s1, r1, s2, r2, s3, r3,
):
    nx, nc, nz, ny = dims
    me = Place(dims)
    per_owner, slab, width = out.shape
    count = left.shape[0]
    strip = ny * slab
    f32, bf16 = jnp.float32, jnp.bfloat16
    size = {"x": nx, "y": ny}
    first = (me.x * nc + me.c) * per_owner

    def rows(z, y):
        return pl.ds((z * ny + y) * slab, slab)

    low, high = pl.ds(0, per_owner // 2), pl.ds(per_owner // 2, per_owner - per_owner // 2)

    def wave(z, e=0, half=low):
        return wave_all.at[half, rows(z, lax.rem(me.y + ny - e, ny)), :]

    def high_y(e):
        return remote(
            wave_ref.at[high], wave(me.z, 0, high), hys.at[e], hyr.at[e], me.device(y=e)
        )

    def high_block(e):
        return lambda z: wave(z, e, high)

    def high_z(e):
        return lambda up, z, src: chain(high_block(e), hzs.at[e], hzr.at[e], up, z, src)

    def base(z, e=0, f=0, g=0):
        x, c, _, y = me.at(x=nx - f, c=nc - g, y=ny - e)
        return base_all.at[pl.ds((x * nc + c) * per_owner, per_owner), rows(z, y), :]

    keep_wave = pltpu.make_async_copy(
        wave_ref, wave_all.at[:, rows(me.z, me.y), :], local.at[0]
    )
    keep_base = pltpu.make_async_copy(base_ref, base(me.z), local.at[1])
    take_left = pltpu.make_async_copy(left_hbm, left, local.at[2])
    take_right = pltpu.make_async_copy(right_hbm, right, local.at[3])

    def chain(block, send, recv, up, z, src):
        shift = 1 if up else nz - 1
        return remote(
            src, block(z), send.at[0 if up else 1, z], recv.at[z], me.device(z=shift)
        )

    def wave_z(up, z, src):
        return chain(wave, wzs, wzr, up, z, src)

    def base_z(up, z, src):
        return chain(base, bzs, bzr, up, z, src)

    def wave_y(z, e, src):
        return remote(src, wave(z), wys.at[e, z], wyr.at[e, z], me.device(y=e))

    def base_y(z, e, src):
        return remote(src, base(z), bys.at[e, z], byr.at[e, z], me.device(y=e))

    def base_x(z, e, f, src):
        return remote(src, base(z, e), bxs.at[f, e, z], bxr.at[f, e, z], me.device(x=f))

    def base_c(z, e, f, g, src):
        return remote(src, base(z, e, f), bcs.at[f, e, z], bcr.at[f, e, z], me.device(c=g))

    def each_far_z(visit):
        for d in range(1, nz):

            @pl.when(me.z >= d)
            def _():
                visit(me.z - d, True)

            @pl.when(me.z + d < nz)
            def _():
                visit(me.z + d, False)

    def both_ways(start, src):
        @pl.when(me.z < nz - 1)
        def _():
            start(True, me.z, src).start()

        @pl.when(me.z > 0)
        def _():
            start(False, me.z, src).start()

    def relay(copy, block, z, up):
        copy(up, z, block(z)).wait_recv()

        @pl.when(me.z < nz - 1 if up else me.z > 0)
        def _():
            copy(up, z, block(z)).start()

    def forward_x(z, e, src):
        for f in range(1, nx):
            base_x(z, e, f, src).start()
        for g in range(1, nc):
            base_c(z, e, 0, g, src).start()

    me.greet()
    for e in range(1, ny):
        high_y(e).start()
    both_ways(wave_z, wave_ref.at[low])
    both_ways(high_z(0), wave_ref.at[high])
    for e in range(1, ny):
        wave_y(me.z, e, wave_ref.at[low]).start()
    keep_wave.start()
    take_left.start()
    take_right.start()
    keep_base.start()
    both_ways(base_z, base_ref)
    forward_x(me.z, 0, base_ref)

    def on_wave(z, up):
        relay(wave_z, wave, z, up)
        for e in range(1, ny):
            wave_y(z, e, wave(z)).start()
        for e in range(ny):
            relay(high_z(e), high_block(e), z, up)

    for e in range(1, ny):
        high_y(e).wait_recv()
        both_ways(high_z(e), wave(me.z, e, high))
    each_far_z(on_wave)
    for e in range(1, ny):
        base_y(me.z, e, base_ref).start()

    def on_base(z, up):
        relay(base_z, base, z, up)
        forward_x(z, 0, base(z))
        for e in range(1, ny):
            base_y(z, e, base(z)).start()

    each_far_z(on_base)
    keep_wave.wait()
    take_left.wait()
    take_right.wait()
    for e in range(1, ny):

        @pl.loop(0, nz)
        def _(z):
            wave_y(z, e, wave(z, e)).wait_recv()

    row = lax.broadcasted_iota(jnp.int32, (width, width), 0)
    column = lax.broadcasted_iota(jnp.int32, (width, width), 1)
    for j in range(per_owner):
        order = order_of(first + j, sector_slot, orders, sectors)
        inside = jnp.maximum(row, column) < order
        masked[j] = jnp.where(inside, wave_all[j], jnp.zeros((), bf16))

    early = min(count // 2, nz)

    def pass_on(i):
        z = lax.rem(me.z + i, nz)
        for e in range(1, ny):
            base_y(z, e, base(z, e)).wait_recv()
            forward_x(z, e, base(z, e))

    @pl.loop(0, count)
    def _(p):
        a = lax.rem(sector_slot[source[p]], per_owner)
        projected = jnp.dot(left[p], masked[a], preferred_element_type=f32)
        product[p] = lax.dot_general(
            projected.astype(bf16), right[p], (((1,), (1,)), ((), ())),
            preferred_element_type=f32,
        )

        @pl.when((lax.rem(p, 2) == 1) & (p < 2 * early))
        def _():
            pass_on(p // 2)

    landed = [sector_slot[target[p]] for p in range(count)]

    def partial_sum(slot, start, size):
        total = None
        for p in range(count):
            weight = jnp.where(landed[p] == slot, 1.0, 0.0).astype(f32)
            term = product[p, pl.ds(start, size), :] * weight
            total = term if total is None else total + term
        return total

    def axes(j):
        return ("x", "y") if j % 2 == 0 else ("y", "x")

    def zq(d):
        return lax.rem(me.z + d, nz)

    def core_copy(x, j, d):
        return remote(
            send_c.at[d, j, x], got_c.at[d, j, x], cs.at[d, j, x], cr.at[d, j, x], me.device(c=1)
        )

    def copy_1(j, d, k):
        return remote(
            send_1.at[d, j, k], got_1.at[d, j, k], s1.at[d, j, k], r1.at[d, j, k],
            me.device(**{axes(j)[0]: k}),
        )

    def copy_2(j, d, k):
        return remote(
            send_2.at[d, j, k], got_2.at[d, j, k], s2.at[d, j, k], r2.at[d, j, k],
            me.device(**{axes(j)[1]: k}),
        )

    def copy_3(j, d):
        return remote(
            send_3.at[d, j], got_3.at[d, j], s3.at[d, j], r3.at[d, j], me.device(z=d)
        )

    def unit(d):
        return lax.rem(d + 1, nz)

    if nc > 1:

        @pl.loop(0, nz)
        def _(i):
            d = unit(i)
            for j in range(per_owner):
                for x in range(nx):
                    slot = (x * nc + lax.rem(me.c + 1, nc)) * per_owner + j
                    for m in range(ny):
                        value = partial_sum(slot, pl.multiple_of(zq(d) * strip + m * slab, slab), slab)
                        send_c[d, j, x, pl.ds(m * slab, slab), :] = value.astype(bf16)
                    core_copy(x, j, d).start()

    @pl.loop(0, nz)
    def _(i):
        d = unit(i)
        for j in range(per_owner):
            n1 = size[axes(j)[0]]
            n2 = size[axes(j)[1]]
            if nc > 1:
                for x in range(nx):
                    core_copy(x, j, d).wait_recv()
            for k in list(range(1, n1)) + [0]:
                for m in range(n2):
                    if axes(j)[0] == "x":
                        x, y = lax.rem(me.x + k, nx), m
                    else:
                        x, y = m, lax.rem(me.y + k, ny)
                    offset = pl.multiple_of(y * slab, slab)
                    slot = (x * nc + me.c) * per_owner + j
                    value = partial_sum(slot, pl.multiple_of(zq(d) * strip + offset, slab), slab)
                    if nc > 1:
                        value = value + got_c[d, j, x, pl.ds(offset, slab), :].astype(f32)
                    if k:
                        send_1[d, j, k, m] = value.astype(bf16)
                    else:
                        mid[d, j, m] = value
                if k:
                    copy_1(j, d, k).start()

    @pl.loop(early, nz)
    def _(i):
        pass_on(i)

    keep_base.wait()
    take_bases = pltpu.make_async_copy(
        base_all.at[pl.ds(first, per_owner)], own_bases, local.at[4]
    )
    take_bases.start()
    take_bases.wait()

    @pl.loop(0, count)
    def _(p):
        a = lax.rem(sector_slot[source[p]], per_owner)
        half[p] = jnp.dot(left[p], own_bases[a], preferred_element_type=f32).astype(bf16)

    give_half = pltpu.make_async_copy(half, half_out, local.at[5])
    give_half.start()

    @pl.loop(0, nz)
    def _(i):
        d = unit(i)
        for j in range(per_owner):
            axis_1, axis_2 = axes(j)
            n1, n2 = size[axis_1], size[axis_2]
            for k in range(1, n1):
                copy_1(j, d, k).wait_recv()
            for h in list(range(1, n2)) + [0]:
                m = lax.rem(getattr(me, axis_2) + h, n2)
                value = mid[d, j, m]
                for k in range(1, n1):
                    value = value + got_1[d, j, k, m].astype(f32)
                if h:
                    send_2[d, j, h] = value.astype(bf16)
                    copy_2(j, d, h).start()
                else:
                    held[d, j] = value

    for f in range(1, nx):
        for e in range(1):

            @pl.loop(0, nz)
            def _(z):
                base_x(z, e, f, base(z, e, f)).wait_recv()
                for g in range(1, nc):
                    base_c(z, e, f, g, base(z, e, f)).start()

    def stage_3(d, j):
        for h in range(1, size[axes(j)[1]]):
            copy_2(j, d, h).wait_recv()
        value = held[d, j]
        for h in range(1, size[axes(j)[1]]):
            value = value + got_2[d, j, h].astype(f32)
        return value

    @pl.loop(1, nz)
    def _(d):
        for j in range(per_owner):
            send_3[d, j] = stage_3(d, j).astype(bf16)
            copy_3(j, d).start()

    for f in range(1, nx):
        for e in range(1, ny):

            @pl.loop(0, nz)
            def _(i):
                z = lax.rem(me.z + i, nz)
                base_x(z, e, f, base(z, e, f)).wait_recv()
                for g in range(1, nc):
                    base_c(z, e, f, g, base(z, e, f)).start()

    row = lax.broadcasted_iota(jnp.int32, (slab, width), 0) + (me.z * ny + me.y) * slab
    column = lax.broadcasted_iota(jnp.int32, (slab, width), 1)
    for j in range(per_owner):
        value = stage_3(0, j)
        for d in range(1, nz):
            copy_3(j, d).wait_recv()
            value = value + got_3[d, j].astype(f32)
        order = order_of(first + j, sector_slot, orders, sectors)
        inside = jnp.maximum(row, column) < order
        out[j] = jnp.where(inside, value, 0.0).astype(out.dtype)

    give_half.wait()
    for e in range(1, ny):
        high_y(e).wait_send()
    relayed = [(wave_z, wave), (base_z, base)] + [(high_z(e), high_block(e)) for e in range(ny)]
    for start, block in relayed:

        @pl.when(me.z < nz - 1)
        def _():
            @pl.loop(0, me.z + 1)
            def _(z):
                start(True, z, block(z)).wait_send()

        @pl.when(me.z > 0)
        def _():
            @pl.loop(me.z, nz)
            def _(z):
                start(False, z, block(z)).wait_send()

    @pl.loop(0, nz)
    def _(z):
        for e in range(1, ny):
            wave_y(z, e, wave(z)).wait_send()
            base_y(z, e, base(z)).wait_send()
        for e in range(ny):
            for f in range(1, nx):
                base_x(z, e, f, base(z, e)).wait_send()
            for f in range(nx):
                for g in range(1, nc):
                    base_c(z, e, f, g, base(z, e, f)).wait()

    @pl.loop(0, nz)
    def _(d):
        for j in range(per_owner):
            if nc > 1:
                for x in range(nx):
                    core_copy(x, j, d).wait_send()
            for k in range(1, size[axes(j)[0]]):
                copy_1(j, d, k).wait_send()
            for h in range(1, size[axes(j)[1]]):
                copy_2(j, d, h).wait_send()

    @pl.loop(1, nz)
    def _(d):
        for j in range(per_owner):
            copy_3(j, d).wait_send()


def sigma_and_bases(
    dims, wavefunction, sector_bases, left, right, source, target, sector_slot, orders
):
    nx, nc, nz, ny = dims
    per_owner, slab, width = wavefunction.shape
    sectors = sector_slot.shape[0]
    most = max(nx, ny)
    dma = pltpu.SemaphoreType.DMA
    bf16, f32 = jnp.bfloat16, jnp.float32
    full = (per_owner, nz * ny * slab, width)
    return pl.pallas_call(
        functools.partial(sigma_kernel, dims, sectors),
        out_shape=(
            jax.ShapeDtypeStruct((per_owner, slab, width), bf16),
            jax.ShapeDtypeStruct((sectors, nz * ny * slab, width), sector_bases.dtype),
            jax.ShapeDtypeStruct(left.shape, bf16),
        ),
        in_specs=[VMEM, VMEM, ANY, ANY, SMEM, SMEM, SMEM, SMEM],
        out_specs=(VMEM, ANY, ANY),
        scratch_shapes=[
            pltpu.VMEM(full, bf16),
            pltpu.VMEM(full, bf16),
            pltpu.VMEM(full, bf16),
            pltpu.VMEM(left.shape, bf16),
            pltpu.VMEM(left.shape, bf16),
            pltpu.VMEM(right.shape, bf16),
            pltpu.VMEM(left.shape, f32),
            pltpu.VMEM((nz, per_owner, nx, ny * slab, width), bf16),
            pltpu.VMEM((nz, per_owner, nx, ny * slab, width), bf16),
            pltpu.VMEM((nz, per_owner, most, most, slab, width), bf16),
            pltpu.VMEM((nz, per_owner, most, most, slab, width), bf16),
            pltpu.VMEM((nz, per_owner, most, slab, width), f32),
            pltpu.VMEM((nz, per_owner, most, slab, width), bf16),
            pltpu.VMEM((nz, per_owner, most, slab, width), bf16),
            pltpu.VMEM((nz, per_owner, slab, width), f32),
            pltpu.VMEM((nz, per_owner, slab, width), bf16),
            pltpu.VMEM((nz, per_owner, slab, width), bf16),
        ]
        + [dma((6,))]
        + [dma((ny,)), dma((ny,)), dma((ny, 2, nz)), dma((ny, nz))]
        + [dma((2, nz)), dma((nz,))] * 2
        + [dma((ny, nz))] * 4
        + [dma((nx, ny, nz))] * 4
        + [dma((nz, per_owner, nx))] * 2
        + [dma((nz, per_owner, most))] * 4
        + [dma((nz, per_owner))] * 2,
        compiler_params=pltpu.CompilerParams(
            collective_id=0, has_side_effects=True, vmem_limit_bytes=60 * 1024 * 1024
        ),
        name="sigma",
    )(wavefunction, sector_bases, left, right, source, target, sector_slot, orders)


def rotate_kernel(target, sector_slot, basis, half, rotated):
    rotated[0] = lax.dot_general(
        basis[0], half[0], (((0,), (0,)), ((), ())), preferred_element_type=jnp.float32
    ).astype(rotated.dtype)


def rotate(bases, half, target, sector_slot):
    count, width, _ = half.shape
    each = pl.BlockSpec((1, width, width), lambda p, *_: (p, 0, 0))
    chosen = pl.BlockSpec((1, width, width), lambda p, target, slot: (slot[target[p]], 0, 0))
    return pl.pallas_call(
        rotate_kernel,
        out_shape=jax.ShapeDtypeStruct(half.shape, half.dtype),
        grid_spec=pltpu.PrefetchScalarGridSpec(
            num_scalar_prefetch=2, grid=(count,), in_specs=[chosen, each], out_specs=each
        ),
        compiler_params=pltpu.CompilerParams(
            dimension_semantics=("arbitrary",), vmem_limit_bytes=60 * 1024 * 1024
        ),
        name="rotate",
    )(target, sector_slot, bases, half)


def solution(mesh):
    dims = grid_of(mesh.shape["sector"], mesh.shape["op"])

    def per_device(
        wavefunction, sector_bases, left_env, right_env, pair_source, pair_target, sector_slot, orders
    ):
        sigma_blocks, bases, half = sigma_and_bases(
            dims, wavefunction, sector_bases, left_env, right_env,
            pair_source, pair_target, sector_slot, orders,
        )
        left_rotated = rotate(bases, half, pair_target, sector_slot)
        return sigma_blocks, left_rotated

    placed = (
        P("sector", "op", None),
        P("sector", "op", None),
        P(("sector", "op"), None, None),
        P(("sector", "op"), None, None),
        P(("sector", "op")),
        P(("sector", "op")),
        P(),
        P(),
    )
    return jax.shard_map(
        per_device,
        mesh=mesh,
        in_specs=placed,
        out_specs=(P("sector", "op", None), P(("sector", "op"), None, None)),
        check_vma=False,
    )
```
